32 devices in a mesh: ckpt: 4 (over z), shard: 8 (over y, x, core).
Axes of the slice: x: 2, y: 2, z: 4, core: 2. Of those that a mesh axis runs over, the one named last changes fastest.
Arguments:
- task_vectors: bfloat16 [4, 4096, 16384], P('ckpt', 'shard'), may hold values from -0.125 to 0.125, as said below
- thresholds: float32 [4], replicated, may hold values from 0.009 to 0.062, as said below
- base_weight: float32 [4096, 16384], P('ckpt', 'shard'), may hold values from -0.3 to 0.3
Outputs:
- merged: float32 [4096, 16384], P('ckpt', 'shard')
The draws below stay inside these ranges and needn't reach their ends.
Inputs may be any that keep to these rules, and one draw needn't show every extreme that they name: `task_vectors`: every entry is a whole multiple of 2^-14. `thresholds`: every threshold is an odd multiple of 2^-15.
All inputs are finite; a program needn't handle non-finite values.
Results may differ from the reference program's by a relative error of at most 0.0003.
Values may be sent and summed in bfloat16 or wider, within the bound.
A program may use at most 128 MiB of HBM per device.

```python
import jax
import jax.numpy as jnp
from jax import lax

D = 4096
FFW = 16384
TASKS = 4


def draw_task_vectors(key, part):
    first_key, second_key = jax.random.split(key, 2)
    steps_count = jax.random.randint(first_key, (TASKS, D, FFW), -255, 256)
    exponent = jax.random.randint(second_key, (TASKS, D, FFW), 0, 4)
    values = steps_count.astype(jnp.float32) * jnp.exp2(exponent.astype(jnp.float32) - 14.0)
    return values.astype(jnp.bfloat16)


def draw_thresholds(key, part):
    middle = jax.random.randint(jax.random.fold_in(key, 11), (TASKS,), 160, 1000)
    return (2 * middle + 1).astype(jnp.float32) / 32768.0


def levels(key, dims, cuts, low, largest):
    level, own = 1.0, jax.random.fold_in(key, 6)
    for axis_at, blocks in cuts:
        draws = jnp.exp(jax.random.uniform(jax.random.fold_in(own, axis_at), (blocks,), jnp.float32, low / len(cuts), largest / len(cuts)))
        level = level * jnp.repeat(draws, dims[axis_at] // blocks).reshape([-1 if axis == axis_at else 1 for axis in range(len(dims))])
    return level


def normal_values(stream_key, extent, deviation, most, shards=(), kind=jnp.bfloat16):
    factor_of = levels(stream_key, extent, shards, -0.22, 0.18) if shards else 1.0
    values = jax.random.normal(stream_key, extent, jnp.float32) * deviation * factor_of
    return jnp.minimum(jnp.maximum(values, -most), most).astype(kind)


def setup_inputs(seed: int = 0) -> dict:
    splits = jax.random.split(jax.random.key(seed), 4)
    task_vectors = draw_task_vectors(jax.random.fold_in(splits[3], 71), 0)
    thresholds = draw_thresholds(jax.random.fold_in(splits[3], 71), 0)
    base_weight = normal_values(splits[2], (D, FFW), 0.05, 0.3, ((0, 4), (1, 8)), jnp.float32)
    return dict(task_vectors=task_vectors, thresholds=thresholds, base_weight=base_weight)


def trim_values(task_block, limit_value):
    values = task_block.astype(jnp.float32)
    return jnp.where(jnp.abs(values) > limit_value, values, jnp.float32(0.0))


def reference(task_vectors, thresholds, base_weight):
    def add_trimmed(running, inputs):
        return running + trim_values(inputs[0], inputs[1]), None

    zeros_block = jnp.zeros(base_weight.shape, jnp.float32)
    signed_total, unused = lax.scan(add_trimmed, zeros_block, (task_vectors, thresholds))

    def add_agreeing(running, inputs):
        trimmed = trim_values(inputs[0], inputs[1])
        agreeing = jnp.logical_or(jnp.logical_and(signed_total > 0, trimmed > 0),
                                  jnp.logical_and(signed_total < 0, trimmed < 0))
        kept_sum = running[0] + jnp.where(agreeing, trimmed, jnp.float32(0.0))
        agree_count = running[1] + agreeing.astype(jnp.float32)
        return (kept_sum, agree_count), None

    (kept_sum, agree_count), unused = lax.scan(add_agreeing, (zeros_block, zeros_block), (task_vectors, thresholds))
    disjoint = jnp.where(agree_count > 0, kept_sum / jnp.maximum(agree_count, 1.0), jnp.float32(0.0))
    return base_weight + disjoint
```

```python
import functools

import jax
import jax.numpy as jnp
from jax import lax
from jax.experimental import pallas as pl
from jax.experimental.pallas import tpu as pltpu
from jax.sharding import PartitionSpec as P

MESH = pl.DeviceIdType.MESH
VMEM_BYTES = 67043328
EDGE_ROWS = 16
EDGE_COLS = 512
MAIN_ROWS = 32
AHEAD = 2
LAG = 2
BLOCK = (16, 256)


class Part:
    def __init__(self, first, rows, cols, width, height, sem):
        self.first, self.rows, self.cols = first, rows, cols
        self.across = width // cols
        self.count = self.across * (height // rows)
        self.sem = sem

    def tile(self, j):
        row = self.first + lax.div(j, self.across) * self.rows
        col = lax.rem(j, self.across) * self.cols
        return pl.multiple_of(row, self.rows if self.first % self.rows == 0 else 16), pl.multiple_of(col, self.cols)

    def at(self, j):
        row, col = self.tile(j)
        return pl.ds(row, self.rows), pl.ds(col, self.cols)


def split(RB, W):
    edge, cols = min(EDGE_ROWS, RB), min(EDGE_COLS, W)
    parts = [Part(0, edge, cols, W, edge, 0)]
    middle = RB - 2 * edge
    main = min(MAIN_ROWS, middle)
    parts.append(Part(edge, main, W, W, middle, parts[0].count))
    parts.append(Part(RB - edge, edge, cols, W, edge, parts[1].sem + parts[1].count))
    return parts


def merge_kernel(
    T, S,
    thr_ref, x_ref, base_ref, buf,
    stage, recv, thr,
    s1_send, s1_recv, s2_send, s2_recv, own_sem, base_sem, thr_sem,
):
    g = S // T
    RB, W = stage.shape[1], stage.shape[2]
    head, main, last = split(RB, W)
    t = lax.axis_index("ckpt")
    s = lax.axis_index("shard")
    mine = lax.div(s, g)
    sign = 2 * lax.rem(mine, 2) - 1
    steps = [0]
    if T > 1:
        steps.append(T // 2)
    for i in range(1, (T + 1) // 2):
        steps += [T - sign * i, T + sign * i]

    def own_copy(p, j):
        rows, cols = p.at(j)
        row, col = p.tile(j)
        src = pl.ds(pl.multiple_of(s * W + col, p.cols), p.cols)
        return pltpu.make_async_copy(x_ref.at[0, rows, src], stage.at[s, rows, cols], own_sem.at[p.sem + j])

    base_in = pltpu.make_async_copy(base_ref, buf, base_sem)
    thr_in = pltpu.make_async_copy(thr_ref, thr, thr_sem)

    def plane_copy(p, j, step, q):
        c = lax.rem(mine + step, T) * g + lax.rem(lax.rem(s, g) + q, g)
        rows, cols = p.at(j)
        row, col = p.tile(j)
        src = pl.ds(pl.multiple_of(c * W + col, p.cols), p.cols)
        return pltpu.make_async_remote_copy(
            src_ref=x_ref.at[0, rows, src],
            dst_ref=stage.at[s, rows, cols],
            send_sem=s1_send,
            recv_sem=s1_recv.at[p.sem + j, mine],
            device_id=(t, c),
            device_id_type=MESH,
        )

    def line_copy(p, j, k):
        rows, cols = p.at(j)
        return pltpu.make_async_remote_copy(
            src_ref=stage.at[pl.ds(k * g, g), rows, cols],
            dst_ref=recv.at[lax.rem(t - k - 1 + T, T), :, rows, cols],
            send_sem=s2_send,
            recv_sem=s2_recv.at[p.sem + j],
            device_id=(k, s),
            device_id_type=MESH,
        )

    def plane_start(p, j):
        for n, step in enumerate(steps[1:] + steps[:1]):
            for q in range(g):
                if n < T - 1 or q:
                    plane_copy(p, j, step, q).start()

    def plane_arrived(p, j, k):
        rows, cols = p.at(j)
        sem = s1_recv.at[p.sem + j, k]
        if g > 1:
            @pl.when(k == mine)
            def _():
                part = stage.at[pl.ds(0, g - 1), rows, cols]
                pltpu.make_async_copy(part, part, sem).wait()

        @pl.when(k == mine)
        def _():
            own_copy(p, j).wait()

        @pl.when(k != mine)
        def _():
            part = stage.at[pl.ds(0, g), rows, cols]
            pltpu.make_async_copy(part, part, sem).wait()

    def order(n):
        half = max(T // 2, 1)
        other = jnp.where(2 * t < T, T - half, 0)
        if n < half:
            return other + lax.rem(mine + n, half)
        return lax.rem(other + half, T) + lax.rem(mine + n, half)

    def line_start(p, j):
        for n in range(T):
            k = order(n)
            plane_arrived(p, j, k)

            @pl.when(k != t)
            def _():
                line_copy(p, j, k).start()

    def mean_tile(p, j):
        limits = [thr[lax.rem(t + d, T)] for d in range(T)]
        row, col = p.tile(j)
        br, bc = min(BLOCK[0], p.rows), min(BLOCK[1], p.cols)
        across = p.cols // bc

        def block(n, carry):
            rows = pl.ds(pl.multiple_of(row + lax.div(n, across) * br, br), br)
            cols = pl.ds(pl.multiple_of(col + lax.rem(n, across) * bc, bc), bc)
            for i in range(g):
                trimmed = []
                for d in range(T):
                    if d == 0:
                        v = stage[t * g + i, rows, cols]
                    else:
                        v = recv[d - 1, i, rows, cols]
                    v = v.astype(jnp.float32)
                    trimmed.append(jnp.where(jnp.abs(v) > limits[d], v, 0.0))
                total = functools.reduce(jnp.add, trimmed)
                kept = jnp.zeros_like(total)
                count = jnp.zeros_like(total)
                for v in trimmed:
                    agree = v * total > 0
                    kept = kept + jnp.where(agree, v, 0.0)
                    count = count + jnp.where(agree, 1.0, 0.0)
                buf[i, rows, cols] = buf[i, rows, cols] + kept / jnp.maximum(count, 1.0)
            return carry

        lax.fori_loop(0, (p.rows // br) * across, block, 0)

    def finish(p, j):
        rows, cols = p.at(j)
        part = recv.at[:, :, rows, cols]
        pltpu.make_async_copy(part, part, s2_recv.at[p.sem + j]).wait()
        mean_tile(p, j)

    def loop(p, body, start=0, stop=None):
        def step(j, carry):
            body(p, j)
            return carry

        lax.fori_loop(start, p.count if stop is None else stop, step, 0)

    def send_plane(p, j):
        own_copy(p, j).start()
        plane_start(p, j)

    def own_start(p, j):
        own_copy(p, j).start()

    thr_in.start()
    loop(head, own_start)

    barrier = pltpu.get_barrier_semaphore()
    for d in range(1, S):
        pl.semaphore_signal(
            barrier, inc=1, device_id=(t, lax.rem(s + d, S)), device_id_type=MESH
        )
    for d in range(1, T):
        pl.semaphore_signal(
            barrier, inc=1, device_id=(lax.rem(t + d, T), s), device_id_type=MESH
        )
    pl.semaphore_wait(barrier, S - 1 + T - 1)

    ahead = min(AHEAD, main.count)
    lag = min(LAG, main.count)
    loop(head, plane_start)
    loop(main, send_plane, 0, ahead)
    base_in.start()
    loop(head, line_start)

    def step(p, j):
        @pl.when(j + ahead < p.count)
        def _():
            send_plane(p, j + ahead)

        @pl.when(j + ahead == p.count)
        def _():
            loop(last, send_plane)

        line_start(p, j)

        @pl.when(j + 1 == lag)
        def _():
            base_in.wait()
            thr_in.wait()
            loop(head, finish)

        @pl.when(j >= lag)
        def _():
            finish(p, j - lag)

    loop(main, step)
    loop(last, line_start)
    loop(main, finish, main.count - lag)
    loop(last, finish)

    part = stage.at[pl.ds(0, S - 1)]
    pltpu.make_async_copy(part, part, s1_send).wait()
    pltpu.make_async_copy(recv, recv, s2_send).wait()


def local(task_vectors, thresholds, base_weight):
    T = lax.axis_size("ckpt")
    S = lax.axis_size("shard")
    RB = task_vectors.shape[1]
    W = task_vectors.shape[2] // S
    g = S // T
    N = sum(p.count for p in split(RB, W))
    merged = pl.pallas_call(
        functools.partial(merge_kernel, T, S),
        out_shape=pltpu.VMEM((g, RB, W), jnp.float32),
        in_specs=[
            pl.BlockSpec(memory_space=pltpu.HBM),
            pl.BlockSpec(memory_space=pltpu.HBM),
            pl.BlockSpec(memory_space=pltpu.HBM),
        ],
        out_specs=pl.BlockSpec(memory_space=pltpu.VMEM),
        scratch_shapes=[
            pltpu.VMEM((S, RB, W), jnp.bfloat16),
            pltpu.VMEM((T - 1, g, RB, W), jnp.bfloat16),
            pltpu.SMEM((T,), jnp.float32),
            pltpu.SemaphoreType.DMA,
            pltpu.SemaphoreType.DMA((N, T)),
            pltpu.SemaphoreType.DMA,
            pltpu.SemaphoreType.DMA((N,)),
            pltpu.SemaphoreType.DMA((N,)),
            pltpu.SemaphoreType.DMA,
            pltpu.SemaphoreType.DMA,
        ],
        compiler_params=pltpu.CompilerParams(
            collective_id=0, has_side_effects=True, vmem_limit_bytes=VMEM_BYTES - g * RB * W * 4
        ),
        name="merge_exchange",
    )(thresholds, task_vectors, base_weight.reshape(g, RB, W))
    return merged.reshape(base_weight.shape)


def solution(mesh):
    placed = (P("ckpt", "shard", None), P(), P("ckpt", "shard"))
    return jax.shard_map(
        local, mesh=mesh, in_specs=placed, out_specs=P("ckpt", "shard"), check_vma=False
    )
```

```python
import functools

import jax
import jax.numpy as jnp
from jax import lax
from jax.experimental import pallas as pl
from jax.experimental.pallas import tpu as pltpu
from jax.sharding import PartitionSpec as P

MESH = pl.DeviceIdType.MESH
VMEM_BYTES = 67043328
EDGE_ROWS = 16
EDGE_COLS = 256
RAMP = 2
MAIN_ROWS = 32
AHEAD = 4
LAG = 5
BLOCK = (16, 256)


class Part:
    def __init__(self, first, rows, cols, width, height, sem):
        self.first, self.rows, self.cols = first, rows, cols
        self.across = width // cols
        self.count = self.across * (height // rows)
        self.sem = sem

    def tile(self, j):
        row = self.first + lax.div(j, self.across) * self.rows
        col = lax.rem(j, self.across) * self.cols
        return pl.multiple_of(row, self.rows if self.first % self.rows == 0 else 16), pl.multiple_of(col, self.cols)

    def at(self, j):
        row, col = self.tile(j)
        return pl.ds(row, self.rows), pl.ds(col, self.cols)


def split(RB, W):
    edge, cols = min(EDGE_ROWS, RB), min(EDGE_COLS, W)
    middle = RB - (2 + RAMP) * edge
    parts, row, sem = [], 0, 0
    for rows, wide, height in (
        (edge, cols, edge),
        (edge, W, RAMP * edge),
        (min(MAIN_ROWS, middle), W, middle),
        (edge, cols, edge),
    ):
        parts.append(Part(row, rows, wide, W, height, sem))
        row, sem = row + height, sem + parts[-1].count
    return parts


def merge_kernel(
    T, S,
    thr_ref, x_ref, base_ref, buf,
    stage, recv, thr,
    s1_send, s1_recv, s2_send, s2_recv, own_sem, base_sem, thr_sem, half_in, all_in,
):
    g = S // T
    RB, W = stage.shape[1], stage.shape[2]
    head, ramp, main, last = split(RB, W)
    t = lax.axis_index("ckpt")
    s = lax.axis_index("shard")
    mine = lax.div(s, g)
    sign = 2 * lax.rem(mine, 2) - 1
    steps = [0]
    if T > 1:
        steps.append(T // 2)
    for i in range(1, (T + 1) // 2):
        steps += [T - sign * i, T + sign * i]

    def own_copy(p, j):
        rows, cols = p.at(j)
        row, col = p.tile(j)
        src = pl.ds(pl.multiple_of(s * W + col, p.cols), p.cols)
        return pltpu.make_async_copy(x_ref.at[0, rows, src], stage.at[s, rows, cols], own_sem.at[p.sem + j])

    base_in = pltpu.make_async_copy(base_ref, buf, base_sem)
    thr_in = pltpu.make_async_copy(thr_ref, thr, thr_sem)

    def plane_copy(p, j, step, q):
        c = lax.rem(mine + step, T) * g + lax.rem(lax.rem(s, g) + q, g)
        rows, cols = p.at(j)
        row, col = p.tile(j)
        src = pl.ds(pl.multiple_of(c * W + col, p.cols), p.cols)
        return pltpu.make_async_remote_copy(
            src_ref=x_ref.at[0, rows, src],
            dst_ref=stage.at[s, rows, cols],
            send_sem=s1_send,
            recv_sem=s1_recv.at[p.sem + j, mine],
            device_id=(t, c),
            device_id_type=MESH,
        )

    def line_copy(p, j, k):
        rows, cols = p.at(j)
        return pltpu.make_async_remote_copy(
            src_ref=stage.at[pl.ds(k * g, g), rows, cols],
            dst_ref=recv.at[lax.rem(t - k - 1 + T, T), :, rows, cols],
            send_sem=s2_send,
            recv_sem=s2_recv.at[p.sem + j],
            device_id=(k, s),
            device_id_type=MESH,
        )

    def plane_start(p, j):
        for n, step in enumerate(steps[1:] + steps[:1]):
            for q in range(g):
                if n < T - 1 or q:
                    plane_copy(p, j, step, q).start()

    def plane_arrived(p, j, k):
        rows, cols = p.at(j)
        sem = s1_recv.at[p.sem + j, k]
        if g > 1:
            @pl.when(k == mine)
            def _():
                part = stage.at[pl.ds(0, g - 1), rows, cols]
                pltpu.make_async_copy(part, part, sem).wait()

        @pl.when(k == mine)
        def _():
            own_copy(p, j).wait()

        @pl.when(k != mine)
        def _():
            part = stage.at[pl.ds(0, g), rows, cols]
            pltpu.make_async_copy(part, part, sem).wait()

    half = T // 2
    low = 2 * t < T
    inner, outer = jnp.where(low, t + 1, t - 1), jnp.where(low, t - 1, t + 1)
    depth = jnp.where(low, t, T - 1 - t)

    def order(n):
        other = jnp.where(low, half, 0)
        if n < half:
            return other + lax.rem(mine + n, half)
        return half - other + lax.rem(mine + n, half)

    def line_start(p, j, ns=range(T)):
        for n in ns:
            k = order(n) if p is head else jnp.where(low, T - 1 - n, n)
            plane_arrived(p, j, k)

            @pl.when(k != t)
            def _():
                line_copy(p, j, k).start()

    def mean_tile(p, j):
        limits = [thr[lax.rem(t + d, T)] for d in range(T)]
        row, col = p.tile(j)
        br, bc = min(BLOCK[0], p.rows), min(BLOCK[1], p.cols)
        across = p.cols // bc

        def block(n, carry):
            rows = pl.ds(pl.multiple_of(row + lax.div(n, across) * br, br), br)
            cols = pl.ds(pl.multiple_of(col + lax.rem(n, across) * bc, bc), bc)
            for i in range(g):
                trimmed = []
                for d in range(T):
                    if d == 0:
                        v = stage[t * g + i, rows, cols]
                    else:
                        v = recv[d - 1, i, rows, cols]
                    v = v.astype(jnp.float32)
                    trimmed.append(jnp.where(jnp.abs(v) > limits[d], v, 0.0))
                total = functools.reduce(jnp.add, trimmed)
                kept = jnp.zeros_like(total)
                count = jnp.zeros_like(total)
                for v in trimmed:
                    agree = v * total > 0
                    kept = kept + jnp.where(agree, v, 0.0)
                    count = count + jnp.where(agree, 1.0, 0.0)
                buf[i, rows, cols] = buf[i, rows, cols] + kept / jnp.maximum(count, 1.0)
            return carry

        lax.fori_loop(0, (p.rows // br) * across, block, 0)

    def finish(p, j):
        rows, cols = p.at(j)
        part = recv.at[:, :, rows, cols]
        pltpu.make_async_copy(part, part, s2_recv.at[p.sem + j]).wait()
        mean_tile(p, j)

    def loop(p, body, start=0, stop=None):
        def step(j, carry):
            body(p, j)
            return carry

        lax.fori_loop(start, p.count if stop is None else stop, step, 0)

    def send_plane(p, j):
        own_copy(p, j).start()
        plane_start(p, j)

    def own_start(p, j):
        own_copy(p, j).start()

    thr_in.start()
    loop(head, own_start)

    barrier = pltpu.get_barrier_semaphore()

    def tell(sem, k):
        pl.semaphore_signal(sem, inc=1, device_id=(k, s), device_id_type=MESH)

    for d in range(1, S):
        pl.semaphore_signal(
            barrier, inc=1, device_id=(t, lax.rem(s + d, S)), device_id_type=MESH
        )

    @pl.when(depth == half - 1)
    def _():
        tell(barrier, inner)

    @pl.when(depth > 0)
    def _():
        tell(barrier, outer)

    pl.semaphore_wait(barrier, S)

    def met():
        @pl.when(depth > 0)
        def _():
            pl.semaphore_wait(half_in, 1)

        @pl.when(depth < half - 1)
        def _():
            tell(half_in, inner)
            pl.semaphore_wait(all_in, 1)

        @pl.when(depth == half - 1)
        def _():
            tell(all_in, inner)
            pl.semaphore_wait(all_in, 1)

        @pl.when(depth > 0)
        def _():
            tell(all_in, outer)

    ahead = min(AHEAD, main.count)
    lag = min(LAG, main.count)
    loop(head, plane_start)
    loop(ramp, send_plane)
    loop(main, send_plane, 0, ahead)
    met()
    loop(head, functools.partial(line_start, ns=range(half)))
    loop(head, functools.partial(line_start, ns=range(half, T)))
    base_in.start()
    loop(ramp, line_start)

    def step(p, j):
        @pl.when(j + ahead < p.count)
        def _():
            send_plane(p, j + ahead)

        @pl.when(j + ahead == p.count)
        def _():
            loop(last, send_plane)

        line_start(p, j)

        @pl.when(j + 1 == lag)
        def _():
            base_in.wait()
            thr_in.wait()
            loop(head, finish)
            loop(ramp, finish)

        @pl.when(j >= lag)
        def _():
            finish(p, j - lag)

    loop(main, step)
    loop(last, functools.partial(line_start, ns=range(1)))
    loop(last, functools.partial(line_start, ns=range(1, T)))
    loop(main, finish, main.count - lag)
    loop(last, finish)

    part = stage.at[pl.ds(0, S - 1)]
    pltpu.make_async_copy(part, part, s1_send).wait()
    pltpu.make_async_copy(recv, recv, s2_send).wait()


def local(task_vectors, thresholds, base_weight):
    T = lax.axis_size("ckpt")
    S = lax.axis_size("shard")
    RB = task_vectors.shape[1]
    W = task_vectors.shape[2] // S
    g = S // T
    N = sum(p.count for p in split(RB, W))
    merged = pl.pallas_call(
        functools.partial(merge_kernel, T, S),
        out_shape=pltpu.VMEM((g, RB, W), jnp.float32),
        in_specs=[
            pl.BlockSpec(memory_space=pltpu.HBM),
            pl.BlockSpec(memory_space=pltpu.HBM),
            pl.BlockSpec(memory_space=pltpu.HBM),
        ],
        out_specs=pl.BlockSpec(memory_space=pltpu.VMEM),
        scratch_shapes=[
            pltpu.VMEM((S, RB, W), jnp.bfloat16),
            pltpu.VMEM((T - 1, g, RB, W), jnp.bfloat16),
            pltpu.SMEM((T,), jnp.float32),
            pltpu.SemaphoreType.DMA,
            pltpu.SemaphoreType.DMA((N, T)),
            pltpu.SemaphoreType.DMA,
            pltpu.SemaphoreType.DMA((N,)),
            pltpu.SemaphoreType.DMA((N,)),
            pltpu.SemaphoreType.DMA,
            pltpu.SemaphoreType.DMA,
            pltpu.SemaphoreType.REGULAR,
            pltpu.SemaphoreType.REGULAR,
        ],
        compiler_params=pltpu.CompilerParams(
            collective_id=0, has_side_effects=True, vmem_limit_bytes=VMEM_BYTES - g * RB * W * 4
        ),
        name="merge_exchange",
    )(thresholds, task_vectors, base_weight.reshape(g, RB, W))
    return merged.reshape(base_weight.shape)


def solution(mesh):
    placed = (P("ckpt", "shard", None), P(), P("ckpt", "shard"))
    return jax.shard_map(
        local, mesh=mesh, in_specs=placed, out_specs=P("ckpt", "shard"), check_vma=False
    )
```
